32 devices in a mesh: lon: 4 (over y, x), lat: 8 (over z, core).
Axes of the slice: x: 2, y: 2, z: 4, core: 2. Of those that a mesh axis runs over, the one named last changes fastest.
Arguments:
- tracer: float32 [1024, 64, 128], P('lon', 'lat'), may hold values from -6 to 6
- offsets: int32 [64], P('lat'), may hold values from 0 to 1023
- frac_lon: float32 [64], P('lat'), may hold values from 0 to 1
- frac_lat: float32 [64], P('lat'), may hold values from 0 to 1
- frac_lev: float32 [64], P('lat'), may hold values from 0 to 1
- metric: float32 [64], P('lat'), may hold values from 0.5 to 2
- vertical_coef: float32 [128], replicated, may hold values from 0.5 to 4
- inverses: float32 [64, 128, 128], P('lat'), may hold values from -0.1 to 0.6, as said below
Outputs:
- advected: float32 [1024, 64, 128], P('lon', 'lat')
- pressure: float32 [1024, 64, 128], P('lon', 'lat')
- residual: float32 [1024, 64, 128], P('lon', 'lat')
The draws below stay inside these ranges and needn't reach their ends.
Inputs may be any that keep to these rules, and one draw needn't show every extreme that they name: `inverses`: one matrix for each latitude row.
All inputs are finite; a program needn't handle non-finite values.
Results may differ from the reference program's by a relative error of at most 0.00016.
Values sent between devices are 32-bit elements; how exact they have to be, the bound alone decides.
A program may use at most 128 MiB of HBM per device.

```python
import math
import jax
import jax.numpy as jnp
from jax import lax

L = 128
ITERS = 3
NX = 1024
NY = 64


def draw_inverses(key, part):
    first_key, second_key = jax.random.split(jax.random.fold_in(key, 7))
    scales = jnp.exp(jax.random.uniform(first_key, (NY,), jnp.float32, jnp.log(0.1), jnp.log(0.5)))
    noise = jnp.clip(jax.random.normal(second_key, (NY, L, L), jnp.float32), -3.0, 3.0)
    identity = jnp.eye(L, dtype=jnp.float32)
    return scales[:, None, None] * (identity[None] + 0.03 * noise)


def set_ends(entries, rng, least, top_value):
    longest = entries.shape.index(max(entries.shape))
    spots = []
    for shift in (0, 1):
        where = [jax.random.randint(jax.random.fold_in(rng, axis), (), 0, length) for axis, length in enumerate(entries.shape)]
        where[longest] = (where[longest] + shift) % entries.shape[longest]
        spots.append(tuple(where))
    return entries.at[spots[0]].set(least).at[spots[1]].set(top_value)


def steps_of(own_key, extent, shards, least, largest):
    loudness = 1.0
    for dim, blocks in shards:
        draws = jax.random.uniform(jax.random.fold_in(jax.random.fold_in(own_key, 6), dim), (blocks,), jnp.float32, least / len(shards), largest / len(shards))
        loudness = loudness * jnp.repeat(jnp.exp(draws), extent[dim] // blocks).reshape((-1,) + (1,) * (len(extent) - 1 - dim))
    return loudness


def normal_values(rng, extent, spread, limit, cuts=(), held_as=jnp.bfloat16):
    entries = jax.random.normal(rng, extent, jnp.float32) * spread
    if len(cuts) > 0:
        entries = steps_of(rng, extent, cuts, -0.22, 0.18) * entries
    return jnp.clip(entries, min=-limit, max=limit).astype(held_as)


def setup_inputs(seed: int = 0) -> dict:
    arg_keys = jax.random.split(jax.random.key(seed), 9)
    tracer = normal_values(arg_keys[0], (NX, NY, L), 1.0, 6.0, ((0, 4), (1, 8)), jnp.float32)
    offsets = set_ends(jax.random.randint(arg_keys[1], (NY,), 0, NX), jax.random.fold_in(arg_keys[1], 1), 0, NX - 1).astype(jnp.int32)
    frac_lon = jnp.clip(1.0 * jax.random.uniform(arg_keys[2], (NY,), jnp.float32) ** steps_of(arg_keys[2], (NY,), ((0, 8),), -0.2, 0.2), 0.0, 1.0)
    frac_lat = jnp.clip(1.0 * jax.random.uniform(arg_keys[3], (NY,), jnp.float32) ** steps_of(arg_keys[3], (NY,), ((0, 8),), -0.2, 0.2), 0.0, 1.0)
    frac_lev = jnp.clip(1.0 * jax.random.uniform(arg_keys[4], (NY,), jnp.float32) ** steps_of(arg_keys[4], (NY,), ((0, 8),), -0.2, 0.2), 0.0, 1.0)
    metric = jnp.clip(jnp.exp(math.log(2.0) - 1.3862944 * jax.random.uniform(arg_keys[5], (NY,), jnp.float32) ** steps_of(arg_keys[5], (NY,), ((0, 8),), -0.2, 0.2)), 0.5, 2.0)
    vertical_coef = jnp.clip(jnp.exp(jax.random.uniform(arg_keys[6], (L,), jnp.float32, math.log(0.5), math.log(4.0))), 0.5, 4.0)
    inverses = draw_inverses(jax.random.fold_in(arg_keys[8], 71), 0)
    return {"tracer": tracer, "offsets": offsets, "frac_lon": frac_lon, "frac_lat": frac_lat, "frac_lev": frac_lev, "metric": metric, "vertical_coef": vertical_coef, "inverses": inverses}


def cubic_weights(fraction):
    return (-fraction * (fraction - 1.0) * (fraction - 2.0) / 6.0,
            (fraction + 1.0) * (fraction - 1.0) * (fraction - 2.0) / 2.0,
            -(fraction + 1.0) * fraction * (fraction - 2.0) / 2.0,
            (fraction + 1.0) * fraction * (fraction - 1.0) / 6.0)


def operate(field, metric, vertical_coef):
    eastern = jnp.roll(field, -1, 0)
    western = jnp.roll(field, 1, 0)
    padded = jnp.pad(field, ((0, 0), (1, 1), (0, 0)))
    levels = jnp.pad(field, ((0, 0), (0, 0), (1, 1)))
    result = metric[None, :, None] * (2.0 * field - eastern - western)
    result = result + (2.0 * field - padded[:, 2:] - padded[:, :-2])
    result = result + vertical_coef[None, None, :] * (2.0 * field - levels[:, :, 2:] - levels[:, :, :-2])
    return result + 0.1 * field


def precondition(inverses, field):
    return jnp.einsum('jkm,xjm->xjk', inverses, field, precision=lax.Precision.HIGHEST)


def reference(tracer, offsets, frac_lon, frac_lat, frac_lev, metric, vertical_coef, inverses):
    lat_weights = cubic_weights(frac_lat)
    padded = jnp.pad(tracer, ((0, 0), (1, 2), (0, 0)))
    lat_mixed = jnp.zeros_like(tracer)
    for tap_index in range(4):
        lat_mixed = lat_mixed + lat_weights[tap_index][None, :, None] * padded[:, tap_index:tap_index + NY]
    lev_weights = cubic_weights(frac_lev)
    padded = jnp.pad(lat_mixed, ((0, 0), (0, 0), (1, 2)))
    lev_mixed = jnp.zeros_like(tracer)
    for tap_index in range(4):
        lev_mixed = lev_mixed + lev_weights[tap_index][None, :, None] * padded[:, :, tap_index:tap_index + L]
    lon_weights = cubic_weights(frac_lon)
    columns = jnp.arange(NX, dtype=jnp.int32)[:, None]
    row_index = jnp.arange(NY, dtype=jnp.int32)[None, :]
    advected = jnp.zeros_like(tracer)
    for tap_index in range(4):
        source = jnp.mod(columns - offsets.astype(jnp.int32)[None, :] + (tap_index - 1), NX).astype(jnp.int32)
        advected = advected + lon_weights[tap_index][None, :, None] * lev_mixed[source, row_index]
    pressure = jnp.zeros_like(advected)
    residual = advected
    first = precondition(inverses, residual)
    directions = [first]
    images = [operate(first, metric, vertical_coef)]
    along = jnp.sum(residual * images[0])
    squares = [jnp.sum(images[0] * images[0])]
    for step in range(ITERS):
        alpha = along / squares[step]
        pressure = pressure + alpha * directions[step]
        residual = residual - alpha * images[step]
        if step + 1 < ITERS:
            search = precondition(inverses, residual)
            image_new = operate(search, metric, vertical_coef)
            direction_new = search
            for prior in range(step + 1):
                factor = -jnp.sum(image_new * images[prior]) / squares[prior]
                direction_new = direction_new + factor * directions[prior]
                image_new = image_new + factor * images[prior]
            directions.append(direction_new)
            images.append(image_new)
            along = jnp.sum(residual * image_new)
            squares.append(jnp.sum(image_new * image_new))
    return advected, pressure, residual
```

```python
import functools

import jax
import jax.numpy as jnp
from jax import lax
from jax.experimental import pallas as pl
from jax.experimental.pallas import tpu as pltpu
from jax.sharding import PartitionSpec as P

ITERS = 3
VM = pl.BlockSpec(memory_space=pltpu.VMEM)
SM = pl.BlockSpec(memory_space=pltpu.SMEM)
F32 = jnp.float32


def cubic_weights(f):
    return (
        -f * (f - 1.0) * (f - 2.0) * (1.0 / 6.0),
        (f + 1.0) * (f - 1.0) * (f - 2.0) * 0.5,
        -(f + 1.0) * f * (f - 2.0) * 0.5,
        (f + 1.0) * f * (f - 1.0) * (1.0 / 6.0),
    )


def shape(*dims):
    return jax.ShapeDtypeStruct(dims, F32)


def mix_kernel(rows, fr_lat, fr_lev, t_ref, prev_ref, next_ref, out_ref):
    width, levels = prev_ref.shape
    lane = lax.broadcasted_iota(jnp.int32, (1, levels), 1)
    row = [prev_ref[...]]
    row += [t_ref[pl.ds(j, width, stride=rows), :] for j in range(2)]
    for j in range(rows):
        if j + 2 < rows:
            row.append(t_ref[pl.ds(j + 2, width, stride=rows), :])
        else:
            row.append(next_ref[j + 2 - rows])
        a = cubic_weights(fr_lat[j])
        b = cubic_weights(fr_lev[j])
        lat = a[0] * row[j] + a[1] * row[j + 1] + a[2] * row[j + 2] + a[3] * row[j + 3]
        total = b[1] * lat
        for m in (-1, 1, 2):
            inside = (lane + m >= 0) & (lane + m < levels)
            weight = jnp.where(inside, b[m + 1], 0.0)
            total = total + weight * pltpu.roll(lat, (-m) % levels, 1)
        out_ref[j] = total


def roll_kernel(rows, cells, out, chunk, off, fr, base, in_ref, out_ref, pad):
    for r in range(rows):
        pad[r, :cells, :] = in_ref[r]
        pad[r, cells:, :] = in_ref[r, : chunk + 8, :]
        w = cubic_weights(fr[r])

        def step(c, carry):
            first = c * chunk
            start = lax.rem(base[0] + first - off[r] - 1 + 2 * cells, cells)
            total = w[0] * pad[r, pl.ds(start, chunk), :]
            for m in range(1, 4):
                total = total + w[m] * pad[r, pl.ds(start + m, chunk), :]
            out_ref[r, pl.ds(pl.multiple_of(first, chunk), chunk), :] = total
            return carry

        lax.fori_loop(0, out // chunk, step, 0)


def split(x):
    high = x.astype(jnp.bfloat16)
    return high, (x - high.astype(F32)).astype(jnp.bfloat16)


def solve_lines(inv, v):
    ih, il = split(inv)
    vh, vl = split(v)
    dot = lambda p, q: lax.dot_general(p, q, (((1,), (1,)), ((), ())), preferred_element_type=F32)
    return dot(vh, ih) + (dot(vh, il) + dot(vl, ih))


def put(refs, j, rows, w):
    w_ref, first, last, low, high = refs
    w_ref[j] = w
    low[j : j + 1, :] = w[:1]
    high[j : j + 1, :] = w[-1:]
    if j == 0:
        first[...] = w
    if j == rows - 1:
        last[...] = w


def line_kernel(rows, inv_ref, r_ref, *outs):
    for j in range(rows):
        put(outs, j, rows, solve_lines(inv_ref[j], r_ref[j]))


def apply_row(j, rows, metric, vc_ref, w_ref, prev, nxt, west, east, pad):
    width, levels = prev.shape
    lane = lax.broadcasted_iota(jnp.int32, (1, levels), 1)
    vc = vc_ref[...]
    up = jnp.where(lane < levels - 1, vc, 0.0)
    down = jnp.where(lane > 0, vc, 0.0)
    w = w_ref[j]
    pad[7:8, :] = west[j : j + 1, :]
    pad[8 : 8 + width, :] = w
    pad[8 + width : 9 + width, :] = east[j : j + 1, :]
    south = prev[...] if j == 0 else w_ref[j - 1]
    north = nxt[...] if j == rows - 1 else w_ref[j + 1]
    m = metric[j]
    result = (2.0 * m + 2.1 + 2.0 * vc) * w
    result = result - m * (pad[9 : 9 + width, :] + pad[7 : 7 + width, :])
    result = result - (south + north)
    result = result - up * pltpu.roll(w, levels - 1, 1)
    return result - down * pltpu.roll(w, 1, 1)


def apply_kernel(rows, metric, vc, inv_ref, w_ref, prev, nxt, west, east, v_ref, *rest):
    outs, pad = rest[:-1], rest[-1]
    for j in range(rows):
        v = apply_row(j, rows, metric, vc, w_ref, prev, nxt, west, east, pad.at[j % 2])
        v_ref[j] = v
        put(outs, j, rows, solve_lines(inv_ref[j], v))


def last_kernel(rows, metric, vc, r_ref, v0_ref, v1_ref, w_ref, prev, nxt, west, east, v_ref, sums, pad):
    levels = prev.shape[1]
    acc = [jnp.zeros((1, levels), F32) for _ in range(9)]
    for j in range(rows):
        v2 = apply_row(j, rows, metric, vc, w_ref, prev, nxt, west, east, pad.at[j % 2])
        v_ref[j] = v2
        r, v0, v1 = r_ref[j], v0_ref[j], v1_ref[j]
        pairs = [(r, v0), (r, v1), (r, v2), (v0, v0), (v0, v1), (v0, v2), (v1, v1), (v1, v2), (v2, v2)]
        for n, (p, q) in enumerate(pairs):
            acc[n] = acc[n] + jnp.sum(p * q, axis=0, keepdims=True)
    for n in range(9):
        sums[n : n + 1, :] = acc[n]
    sums[9:, :] = jnp.zeros((7, levels), F32)


def coefficients(t):
    right = t[:3]
    gram = [[t[3], t[4], t[5]], [t[4], t[6], t[7]], [t[5], t[7], t[8]]]
    zero = jnp.zeros_like(t[0])

    def form(p, q):
        total = zero
        for k in range(3):
            for l in range(3):
                if p[k] is not None and q[l] is not None:
                    total = total + p[k] * q[l] * gram[k][l]
        return total

    def add(p, s, q):
        return [x if y is None else (s * y if x is None else x + s * y) for x, y in zip(p, q)]

    q = [[zero + 1.0, None, None]]
    rho, pi = [None] * 3, [None] * 3
    squares = [form(q[0], q[0])]
    for i in range(ITERS):
        along = form(q[i], rho)
        for k in range(3):
            if q[i][k] is not None:
                along = along + q[i][k] * right[k]
        alpha = along / squares[i]
        pi = add(pi, alpha, q[i])
        rho = add(rho, -alpha, q[i])
        if i + 1 < ITERS:
            z = [zero + 1.0, rho[0], rho[1]]
            new = z
            for l in range(i + 1):
                new = add(new, -form(z, q[l]) / squares[l], q[l])
            q.append(new)
            squares.append(form(new, new))
    return rho, pi


def final_kernel(rows, all_ref, r_ref, v0, v1, v2, w0, w1, w2, a_out, p_out, r_out):
    width = r_ref.shape[1]
    total = jnp.sum(jnp.sum(all_ref[...], axis=0), axis=1, keepdims=True)
    rho, pi = coefficients([total[n : n + 1, :] for n in range(9)])
    for j in range(rows):
        r = r_ref[j]
        where = pl.ds(j, width, stride=rows)
        a_out[where, :] = r
        p_out[where, :] = pi[0] * w0[j] + pi[1] * w1[j] + pi[2] * w2[j]
        r_out[where, :] = r + (rho[0] * v0[j] + rho[1] * v1[j] + rho[2] * v2[j])


def call(kernel, outs, ins, scratch=()):
    return pl.pallas_call(
        kernel,
        out_shape=outs,
        in_specs=ins,
        out_specs=jax.tree.map(lambda _: VM, outs),
        scratch_shapes=list(scratch),
    )


def body(tracer, offsets, frac_lon, frac_lat, frac_lev, metric, vertical_coef, inverses):
    width, rows, levels = tracer.shape
    lons, lats = lax.axis_size("lon"), lax.axis_size("lat")
    cells = width * lons
    up = [(i, i + 1) for i in range(lats - 1)]
    down = [(i + 1, i) for i in range(lats - 1)]
    east = [(i, (i + 1) % lons) for i in range(lons)]
    west = [((i + 1) % lons, i) for i in range(lons)]
    flat = tracer.reshape(width * rows, levels)
    prev = lax.ppermute(tracer[:, rows - 1, :], "lat", up)
    nxt = lax.ppermute(jnp.stack([tracer[:, 0, :], tracer[:, 1, :]]), "lat", down)
    cube = shape(rows, width, levels)
    mixed = call(functools.partial(mix_kernel, rows), cube, [SM, SM, VM, VM, VM])(
        frac_lat, frac_lev, flat, prev, nxt
    )
    chunk = min(128, width)
    lon = lax.axis_index("lon")
    if rows % lons == 0:
        some = rows // lons
        piece = lax.all_to_all(mixed, "lon", 0, 1, tiled=True)
        mine = lambda x: lax.dynamic_slice_in_dim(x, lon * some, some)
        args = (mine(offsets), mine(frac_lon), jnp.zeros((1,), jnp.int32))
        out = cells
    else:
        some = rows
        piece = lax.all_gather(mixed, "lon", axis=1, tiled=True)
        args = (offsets, frac_lon, (lon * width).reshape(1).astype(jnp.int32))
        out = width
    turned = call(
        functools.partial(roll_kernel, some, cells, out, chunk),
        shape(some, out, levels),
        [SM, SM, SM, VM],
        [pltpu.VMEM((some, cells + chunk + 8, levels), F32)],
    )(*args, piece)
    if rows % lons == 0:
        turned = lax.all_to_all(turned, "lon", 1, 0, tiled=True)
    r0 = turned
    vc = vertical_coef.reshape(1, levels)
    edge, end = shape(width, levels), shape(rows, levels)
    fields = [cube, edge, edge, end, end]
    pad = [pltpu.VMEM((2, width + 16, levels), F32)]

    def halo(first, last, low, high):
        return (
            lax.ppermute(last, "lat", up),
            lax.ppermute(first, "lat", down),
            lax.ppermute(high, "lon", east),
            lax.ppermute(low, "lon", west),
        )

    w0, *edges = call(functools.partial(line_kernel, rows), fields, [VM, VM])(inverses, r0)
    step = call(functools.partial(apply_kernel, rows), [cube] + fields, [SM] + [VM] * 7, pad)
    v0, w1, *edges = step(metric, vc, inverses, w0, *halo(*edges))
    v1, w2, *edges = step(metric, vc, inverses, w1, *halo(*edges))
    v2, sums = call(
        functools.partial(last_kernel, rows), [cube, shape(16, levels)], [SM] + [VM] * 9, pad
    )(metric, vc, r0, v0, v1, w2, *halo(*edges))
    every = lax.all_gather(sums, ("lon", "lat"))
    whole = shape(width * rows, levels)
    outs = call(functools.partial(final_kernel, rows), [whole] * 3, [VM] * 8)(
        every, r0, v0, v1, v2, w0, w1, w2
    )
    return tuple(x.reshape(width, rows, levels) for x in outs)


def solution(mesh):
    cube = P("lon", "lat", None)
    in_specs = (cube, P("lat"), P("lat"), P("lat"), P("lat"), P("lat"), P(), P("lat", None, None))
    return jax.shard_map(
        body, mesh=mesh, in_specs=in_specs, out_specs=(cube, cube, cube), check_vma=False
    )
```

```python
import functools

import jax
import jax.numpy as jnp
from jax import lax
from jax.experimental import pallas as pl
from jax.experimental.pallas import tpu as pltpu
from jax.sharding import PartitionSpec as P

ITERS = 3
VM = pl.BlockSpec(memory_space=pltpu.VMEM)
SM = pl.BlockSpec(memory_space=pltpu.SMEM)
F32 = jnp.float32


def cubic_weights(f):
    return (
        -f * (f - 1.0) * (f - 2.0) * (1.0 / 6.0),
        (f + 1.0) * (f - 1.0) * (f - 2.0) * 0.5,
        -(f + 1.0) * f * (f - 2.0) * 0.5,
        (f + 1.0) * f * (f - 1.0) * (1.0 / 6.0),
    )


def shape(*dims):
    return jax.ShapeDtypeStruct(dims, F32)


def greet(peers):
    barrier = pltpu.get_barrier_semaphore()
    for peer in peers:
        pl.semaphore_signal(barrier, inc=1, device_id=peer, device_id_type=pl.DeviceIdType.MESH)
    pl.semaphore_wait(barrier, len(peers))


def send(src, dst, send_sem, recv_sem, peer):
    copy = pltpu.make_async_remote_copy(
        src_ref=src,
        dst_ref=dst,
        send_sem=send_sem,
        recv_sem=recv_sem,
        device_id=peer,
        device_id_type=pl.DeviceIdType.MESH,
    )
    copy.start()
    return copy


def around(axis, count, k):
    return {axis: lax.rem(lax.axis_index(axis) + (k + count), count)}


def exchange_kernel(moves, counts, *refs):
    n = len(moves)
    ins, outs, send_sem, recv_sem = refs[:n], refs[n : 2 * n], refs[-2], refs[-1]
    peers = [around(axis, counts[axis], k) for axis, k in moves]
    greet(peers)
    copies = [send(ins[i], outs[i], send_sem.at[i], recv_sem.at[i], peers[i]) for i in range(n)]
    for copy in copies:
        copy.wait()


def turn_kernel(count, some, width, back, x_ref, out_ref, send_sem, recv_sem, own_sem):
    me = lax.axis_index("lon")

    def rows_at(ref, d):
        return ref.at[pl.ds(d * some, some)]

    def cells_at(ref, d):
        return ref.at[:, pl.ds(pl.multiple_of(d * width, width), width), :]

    take, give = (cells_at, rows_at) if back else (rows_at, cells_at)
    own = pltpu.make_async_copy(take(x_ref, me), give(out_ref, me), own_sem)
    own.start()
    peers = [around("lon", count, k) for k in range(1, count)]
    greet(peers)
    copies = [
        send(take(x_ref, p["lon"]), give(out_ref, me), send_sem.at[i], recv_sem.at[i], p)
        for i, p in enumerate(peers)
    ]
    for copy in copies:
        copy.wait()
    own.wait()


def collect_kernel(lons, lats, x_ref, out_ref, send_sem, recv_sem, own_sem):
    a, b = lax.axis_index("lon"), lax.axis_index("lat")
    own = pltpu.make_async_copy(x_ref, out_ref.at[a, b], own_sem)
    own.start()
    first = [around("lat", lats, k) for k in range(1, lats)]
    second = [around("lon", lons, k) for k in range(1, lons)]
    greet(first + second)
    copies = [
        send(x_ref, out_ref.at[a, b], send_sem.at[i], recv_sem.at[i], p) for i, p in enumerate(first)
    ]
    for copy in copies:
        copy.wait()
    own.wait()
    copies = [
        send(out_ref.at[a], out_ref.at[a], send_sem.at[lats - 1 + i], recv_sem.at[lats - 1 + i], p)
        for i, p in enumerate(second)
    ]
    for copy in copies:
        copy.wait()


def talk(kernel, outs, n_in, sems, number, own):
    dma = pltpu.SemaphoreType.DMA
    return pl.pallas_call(
        kernel,
        out_shape=outs,
        in_specs=[VM] * n_in,
        out_specs=jax.tree.map(lambda _: VM, outs),
        scratch_shapes=[dma((sems,)), dma((sems,))] + [dma] * own,
        compiler_params=pltpu.CompilerParams(collective_id=number, has_side_effects=True),
    )


def mix_kernel(rows, keep, fr_lat, fr_lev, t_ref, prev_ref, next_ref, out_ref):
    width, levels = prev_ref.shape
    lane = lax.broadcasted_iota(jnp.int32, (1, levels), 1)
    row = [keep[0] * prev_ref[...]]
    row += [t_ref[pl.ds(j, width, stride=rows), :] for j in range(2)]
    for j in range(rows):
        if j + 2 < rows:
            row.append(t_ref[pl.ds(j + 2, width, stride=rows), :])
        else:
            row.append(keep[1] * next_ref[j + 2 - rows])
        a = cubic_weights(fr_lat[j])
        b = cubic_weights(fr_lev[j])
        lat = a[0] * row[j] + a[1] * row[j + 1] + a[2] * row[j + 2] + a[3] * row[j + 3]
        total = b[1] * lat
        for m in (-1, 1, 2):
            inside = (lane + m >= 0) & (lane + m < levels)
            weight = jnp.where(inside, b[m + 1], 0.0)
            total = total + weight * pltpu.roll(lat, (-m) % levels, 1)
        out_ref[j] = total


def roll_kernel(rows, cells, out, chunk, off, fr, base, in_ref, out_ref, pad):
    for r in range(rows):
        pad[r, :cells, :] = in_ref[r]
        pad[r, cells:, :] = in_ref[r, : chunk + 8, :]
        w = cubic_weights(fr[r])

        def step(c, carry):
            first = c * chunk
            start = lax.rem(base[0] + first - off[r] - 1 + 2 * cells, cells)
            total = w[0] * pad[r, pl.ds(start, chunk), :]
            for m in range(1, 4):
                total = total + w[m] * pad[r, pl.ds(start + m, chunk), :]
            out_ref[r, pl.ds(pl.multiple_of(first, chunk), chunk), :] = total
            return carry

        lax.fori_loop(0, out // chunk, step, 0)


def split(x):
    high = x.astype(jnp.bfloat16)
    return high, (x - high.astype(F32)).astype(jnp.bfloat16)


def solve_lines(inv, v):
    ih, il = split(inv)
    vh, vl = split(v)
    dot = lambda p, q: lax.dot_general(p, q, (((1,), (1,)), ((), ())), preferred_element_type=F32)
    return dot(vh, ih) + (dot(vh, il) + dot(vl, ih))


def put(refs, j, rows, w):
    w_ref, first, last, low, high = refs
    w_ref[j] = w
    low[j : j + 1, :] = w[:1]
    high[j : j + 1, :] = w[-1:]
    if j == 0:
        first[...] = w
    if j == rows - 1:
        last[...] = w


def line_kernel(rows, inv_ref, r_ref, *outs):
    for j in range(rows):
        put(outs, j, rows, solve_lines(inv_ref[j], r_ref[j]))


def apply_row(j, rows, keep, metric, vc_ref, w_ref, prev, nxt, west, east, pad):
    width, levels = prev.shape
    lane = lax.broadcasted_iota(jnp.int32, (1, levels), 1)
    vc = vc_ref[...]
    up = jnp.where(lane < levels - 1, vc, 0.0)
    down = jnp.where(lane > 0, vc, 0.0)
    w = w_ref[j]
    pad[7:8, :] = west[j : j + 1, :]
    pad[8 : 8 + width, :] = w
    pad[8 + width : 9 + width, :] = east[j : j + 1, :]
    south = keep[0] * prev[...] if j == 0 else w_ref[j - 1]
    north = keep[1] * nxt[...] if j == rows - 1 else w_ref[j + 1]
    m = metric[j]
    result = (2.0 * m + 2.1 + 2.0 * vc) * w
    result = result - m * (pad[9 : 9 + width, :] + pad[7 : 7 + width, :])
    result = result - (south + north)
    result = result - up * pltpu.roll(w, levels - 1, 1)
    return result - down * pltpu.roll(w, 1, 1)


def apply_kernel(rows, keep, metric, vc, inv_ref, w_ref, prev, nxt, west, east, v_ref, *rest):
    outs, pad = rest[:-1], rest[-1]
    for j in range(rows):
        v = apply_row(j, rows, keep, metric, vc, w_ref, prev, nxt, west, east, pad.at[j % 2])
        v_ref[j] = v
        put(outs, j, rows, solve_lines(inv_ref[j], v))


def last_kernel(rows, keep, metric, vc, r_ref, v0_ref, v1_ref, w_ref, prev, nxt, west, east, v_ref, sums, pad):
    levels = prev.shape[1]
    acc = [jnp.zeros((1, levels), F32) for _ in range(9)]
    for j in range(rows):
        v2 = apply_row(j, rows, keep, metric, vc, w_ref, prev, nxt, west, east, pad.at[j % 2])
        v_ref[j] = v2
        r, v0, v1 = r_ref[j], v0_ref[j], v1_ref[j]
        pairs = [(r, v0), (r, v1), (r, v2), (v0, v0), (v0, v1), (v0, v2), (v1, v1), (v1, v2), (v2, v2)]
        for n, (p, q) in enumerate(pairs):
            acc[n] = acc[n] + jnp.sum(p * q, axis=0, keepdims=True)
    for n in range(9):
        sums[n : n + 1, :] = acc[n]
    sums[9:, :] = jnp.zeros((7, levels), F32)


def coefficients(t):
    right = t[:3]
    gram = [[t[3], t[4], t[5]], [t[4], t[6], t[7]], [t[5], t[7], t[8]]]
    zero = jnp.zeros_like(t[0])

    def form(p, q):
        total = zero
        for k in range(3):
            for l in range(3):
                if p[k] is not None and q[l] is not None:
                    total = total + p[k] * q[l] * gram[k][l]
        return total

    def add(p, s, q):
        return [x if y is None else (s * y if x is None else x + s * y) for x, y in zip(p, q)]

    q = [[zero + 1.0, None, None]]
    rho, pi = [None] * 3, [None] * 3
    squares = [form(q[0], q[0])]
    for i in range(ITERS):
        along = form(q[i], rho)
        for k in range(3):
            if q[i][k] is not None:
                along = along + q[i][k] * right[k]
        alpha = along / squares[i]
        pi = add(pi, alpha, q[i])
        rho = add(rho, -alpha, q[i])
        if i + 1 < ITERS:
            z = [zero + 1.0, rho[0], rho[1]]
            new = z
            for l in range(i + 1):
                new = add(new, -form(z, q[l]) / squares[l], q[l])
            q.append(new)
            squares.append(form(new, new))
    return rho, pi


def final_kernel(rows, all_ref, r_ref, v0, v1, v2, w0, w1, w2, a_out, p_out, r_out):
    width = r_ref.shape[1]
    total = jnp.sum(jnp.sum(all_ref[...], axis=0), axis=1, keepdims=True)
    rho, pi = coefficients([total[n : n + 1, :] for n in range(9)])
    for j in range(rows):
        r = r_ref[j]
        where = pl.ds(j, width, stride=rows)
        a_out[where, :] = r
        p_out[where, :] = pi[0] * w0[j] + pi[1] * w1[j] + pi[2] * w2[j]
        r_out[where, :] = r + (rho[0] * v0[j] + rho[1] * v1[j] + rho[2] * v2[j])


def call(kernel, outs, ins, scratch=()):
    return pl.pallas_call(
        kernel,
        out_shape=outs,
        in_specs=ins,
        out_specs=jax.tree.map(lambda _: VM, outs),
        scratch_shapes=list(scratch),
    )


def body(tracer, offsets, frac_lon, frac_lat, frac_lev, metric, vertical_coef, inverses):
    width, rows, levels = tracer.shape
    lons, lats = lax.axis_size("lon"), lax.axis_size("lat")
    cells = width * lons
    counts = {"lon": lons, "lat": lats}
    lat = lax.axis_index("lat")
    keep = jnp.stack([lat > 0, lat < lats - 1]).astype(F32)

    def exchange(number, arrays, moves):
        kernel = functools.partial(exchange_kernel, moves, counts)
        outs = [shape(*x.shape) for x in arrays]
        return talk(kernel, outs, len(arrays), len(arrays), number, 0)(*arrays)

    flat = tracer.reshape(width * rows, levels)
    ends = (tracer[:, rows - 1, :], jnp.stack([tracer[:, 0, :], tracer[:, 1, :]]))
    prev, nxt = exchange(1, ends, (("lat", 1), ("lat", -1)))
    cube = shape(rows, width, levels)
    mixed = call(functools.partial(mix_kernel, rows), cube, [SM, SM, SM, VM, VM, VM])(
        keep, frac_lat, frac_lev, flat, prev, nxt
    )
    chunk = min(128, width)
    lon = lax.axis_index("lon")
    if rows % lons == 0:
        some = rows // lons
        turn = functools.partial(turn_kernel, lons, some, width)
        turned_shape = shape(some, cells, levels)
        piece = talk(functools.partial(turn, False), turned_shape, 1, lons - 1, 2, 1)(mixed)
        mine = lambda x: lax.dynamic_slice_in_dim(x, lon * some, some)
        args = (mine(offsets), mine(frac_lon), jnp.zeros((1,), jnp.int32))
        out = cells
    else:
        some = rows
        piece = lax.all_gather(mixed, "lon", axis=1, tiled=True)
        args = (offsets, frac_lon, (lon * width).reshape(1).astype(jnp.int32))
        out = width
    turned = call(
        functools.partial(roll_kernel, some, cells, out, chunk),
        shape(some, out, levels),
        [SM, SM, SM, VM],
        [pltpu.VMEM((some, cells + chunk + 8, levels), F32)],
    )(*args, piece)
    if rows % lons == 0:
        turned = talk(functools.partial(turn, True), cube, 1, lons - 1, 3, 1)(turned)
    r0 = turned
    vc = vertical_coef.reshape(1, levels)
    edge, end = shape(width, levels), shape(rows, levels)
    fields = [cube, edge, edge, end, end]
    pad = [pltpu.VMEM((2, width + 16, levels), F32)]

    moves = (("lat", -1), ("lat", 1), ("lon", -1), ("lon", 1))

    def halo(number, first, last, low, high):
        nxt, prev, east, west = exchange(number, (first, last, low, high), moves)
        return prev, nxt, west, east

    w0, *edges = call(functools.partial(line_kernel, rows), fields, [VM, VM])(inverses, r0)
    step = call(functools.partial(apply_kernel, rows), [cube] + fields, [SM, SM] + [VM] * 7, pad)
    v0, w1, *edges = step(keep, metric, vc, inverses, w0, *halo(4, *edges))
    v1, w2, *edges = step(keep, metric, vc, inverses, w1, *halo(5, *edges))
    v2, sums = call(
        functools.partial(last_kernel, rows), [cube, shape(16, levels)], [SM, SM] + [VM] * 9, pad
    )(keep, metric, vc, r0, v0, v1, w2, *halo(6, *edges))
    collect = functools.partial(collect_kernel, lons, lats)
    every = talk(collect, shape(lons, lats, 16, levels), 1, lons + lats - 2, 7, 1)(sums)
    every = every.reshape(lons * lats, 16, levels)
    whole = shape(width * rows, levels)
    outs = call(functools.partial(final_kernel, rows), [whole] * 3, [VM] * 8)(
        every, r0, v0, v1, v2, w0, w1, w2
    )
    return tuple(x.reshape(width, rows, levels) for x in outs)


def solution(mesh):
    cube = P("lon", "lat", None)
    in_specs = (cube, P("lat"), P("lat"), P("lat"), P("lat"), P("lat"), P(), P("lat", None, None))
    return jax.shard_map(
        body, mesh=mesh, in_specs=in_specs, out_specs=(cube, cube, cube), check_vma=False
    )
```
